256 devices in a mesh: island: 4 (over x), fsdp: 64 (over y, z, core).
Axes of the slice: x: 4, y: 4, z: 8, core: 2. Of those that a mesh axis runs over, the one named last changes fastest.
Arguments:
- pseudo_grad: bfloat16 [4, 14336, 4096], P('island', 'fsdp'), may hold values from -110 to 110
- error_buffer: bfloat16 [4, 14336, 4096], P('island', 'fsdp'), may hold values from -3 to 3
- basis_init: float32 [4096, 64], replicated, may hold values from -6 to 6
- params: float32 [14336, 4096], P(('fsdp', 'island')), may hold values from -6 to 6
- momentum: float32 [14336, 4096], P(('fsdp', 'island')), may hold values from -6 to 6
Outputs:
- new_error: bfloat16 [4, 14336, 4096], P('island', 'fsdp')
- new_params: float32 [14336, 4096], P(('fsdp', 'island'))
- new_momentum: float32 [14336, 4096], P(('fsdp', 'island'))
The draws below stay inside these ranges and needn't reach their ends.
All inputs are finite; a program needn't handle non-finite values.
Results may differ from the reference program's by a relative error of at most 0.0051.
Values sent between devices are 32-bit elements; how exact they have to be, the bound alone decides.
No kernel may reach another device: no remote copies, remote signals or barrier semaphores. Data moves between devices by JAX's collectives and lax.ppermute only.
A program may use at most 64 MiB of HBM per device.

```python
import math
import jax
import jax.numpy as jnp
from jax import lax

D = 4096
FF = 14336
R = 64
ITERS = 4
ISLANDS = 4


def draw_pseudo_grad(key, part):
    subkeys = jax.random.split(key, 3)
    position = jnp.arange(FF, dtype=jnp.float32) / FF
    row_scale = jnp.exp(math.log(3.0) * position + math.log(4.0) * jax.random.uniform(subkeys[1], (FF,), jnp.float32))
    column_scale = jnp.exp(math.log(3.0) * jax.random.uniform(subkeys[2], (D,), jnp.float32))
    island_scale = jnp.exp(math.log(3.0) * jnp.arange(ISLANDS, dtype=jnp.float32) / max(ISLANDS - 1, 1))
    fluctuation = jnp.clip(jax.random.normal(subkeys[0], (ISLANDS, FF, D), jnp.float32), -4.0, 4.0)
    result = 0.1 * fluctuation * row_scale[None, :, None] * column_scale[None, None, :] * island_scale[:, None, None]
    return result.astype(jnp.bfloat16)


def level_of(key, extent, cuts, smallest, high):
    level = 1.0
    for dim, blocks in cuts:
        steps = jax.random.uniform(jax.random.fold_in(jax.random.fold_in(key, 6), dim), (blocks,), jnp.float32, smallest / len(cuts), high / len(cuts))
        level = level * jnp.repeat(jnp.exp(steps), extent[dim] // blocks).reshape((-1,) + (1,) * (len(extent) - 1 - dim))
    return level


def noise(own_key, extent, deviation, reach, pieces=(), kind=jnp.bfloat16):
    gain = level_of(own_key, extent, pieces, -0.22, 0.18) if pieces else 1.0
    values = jax.random.normal(own_key, extent, jnp.float32) * deviation * gain
    return jnp.minimum(jnp.maximum(values, -reach), reach).astype(kind)


def setup_inputs(seed: int = 0) -> dict:
    splits = jax.random.split(jax.random.key(seed), 6)
    pseudo_grad = draw_pseudo_grad(jax.random.fold_in(splits[5], 71), 0)
    error_buffer = noise(splits[1], (ISLANDS, FF, D), 0.5, 3.0, ((0, 4), (1, 64)))
    basis_init = noise(splits[2], (D, R), 1.0, 6.0, (), jnp.float32)
    params = noise(splits[3], (FF, D), 1.0, 6.0, ((0, 256),), jnp.float32)
    momentum = noise(splits[4], (FF, D), 1.0, 6.0, ((0, 256),), jnp.float32)
    return dict(pseudo_grad=pseudo_grad, error_buffer=error_buffer, basis_init=basis_init, params=params, momentum=momentum)


momentum_coef = 0.9
outer_rate = 0.7

def reference(pseudo_grad, error_buffer, basis_init, params, momentum):
    combined = (pseudo_grad.astype(jnp.float32) + error_buffer.astype(jnp.float32)).astype(jnp.bfloat16)
    wide = combined.astype(jnp.float32)
    summed = jnp.sum(wide, axis=0)
    right_basis = basis_init
    for sweep in range(ITERS):
        sketch = jnp.dot(summed.astype(jnp.float32), right_basis.astype(jnp.float32), precision=lax.Precision.HIGHEST, preferred_element_type=jnp.float32)
        gram = jnp.dot(sketch.T.astype(jnp.float32), sketch.astype(jnp.float32), precision=lax.Precision.HIGHEST, preferred_element_type=jnp.float32)
        factor = jnp.linalg.cholesky(gram)
        orthonormal = lax.linalg.triangular_solve(factor, sketch, left_side=False, lower=True, transpose_a=True)
        right_basis = jnp.dot(summed.T.astype(jnp.float32), orthonormal.astype(jnp.float32), precision=lax.Precision.HIGHEST, preferred_element_type=jnp.float32)
    approx = jnp.dot(orthonormal.astype(jnp.float32), right_basis.T.astype(jnp.float32), precision=lax.Precision.HIGHEST, preferred_element_type=jnp.float32) * (1.0 / ISLANDS)
    new_error = (wide - approx[None]).astype(jnp.bfloat16)
    new_momentum = momentum_coef * momentum + approx
    new_params = params - outer_rate * (approx + momentum_coef * new_momentum)
    return (new_error, new_params, new_momentum)
```

```python
import jax
import jax.numpy as jnp
from jax import lax
from jax.sharding import Mesh, PartitionSpec as P

ITERS = 4
momentum_coef = 0.9
outer_rate = 0.7
ROW = ("y", "z", "c")


def dot(a, b, ca, cb):
    return lax.dot_general(
        a,
        b,
        (((ca,), (cb,)), ((), ())),
        precision=lax.Precision.HIGHEST,
        preferred_element_type=jnp.float32,
    )


def ring(n, step):
    return [(i, (i + step) % n) for i in range(n)]


def island_parts(v):
    return [v] + [lax.ppermute(v, "x", ring(4, s)) for s in (1, 2, 3)]


def island_sum(v):
    a, b, c, d = island_parts(v)
    return (a + c) + (b + d)


def whiten(gram):
    factor = jnp.linalg.cholesky(gram, symmetrize_input=False)
    eye = jnp.eye(gram.shape[0], dtype=gram.dtype)
    inverse = lax.linalg.triangular_solve(factor, eye, left_side=True, lower=True)
    return inverse.T


def pack(v):
    h = v.shape[0] // 2
    return jnp.concatenate([v[:h], v[h:]], axis=1)


def unpack(v):
    h = v.shape[1] // 2
    return jnp.concatenate([v[:, :h], v[:, h:]], axis=0)


def row_sum(v):
    n = lax.axis_size(ROW)
    packed = pack(v)
    parts = packed.reshape(n, packed.shape[0] // n, packed.shape[1])
    own = jnp.sum(lax.all_to_all(parts, ROW, 0, 0), axis=0)
    full = lax.all_to_all(jnp.broadcast_to(own, parts.shape), ROW, 0, 0)
    return unpack(full.reshape(packed.shape))


def shards(pseudo_grad, error_buffer, basis_init, params, momentum):
    combined = (pseudo_grad[0].astype(jnp.float32) + error_buffer[0].astype(jnp.float32)).astype(
        jnp.bfloat16
    )
    wide = combined.astype(jnp.float32)
    rows, cols = combined.shape
    quarter = params.shape[0]
    rank = basis_init.shape[1]
    islands = lax.axis_size("x")
    me = lax.axis_index("x")
    width = cols // islands

    blocks = jnp.stack([wide[:, i * width : (i + 1) * width] for i in range(islands)])
    total = jnp.sum(lax.all_to_all(blocks, "x", 0, 0), axis=0)

    basis = lax.dynamic_slice_in_dim(basis_init, me * width, width, 0)
    image = island_sum(dot(total, basis, 1, 0))
    right = row_sum(dot(total, image, 0, 0))
    for sweep in range(1, ITERS):
        part = jnp.concatenate([dot(total, right, 1, 0), dot(basis, right, 0, 0)], axis=0)
        both = island_sum(part)
        image, gram = both[:rows], both[rows:]
        raw = dot(total, image, 0, 0)
        scale = whiten(gram)
        basis = dot(right, scale, 1, 0)
        right = dot(row_sum(raw), scale, 1, 0)
    gram = island_sum(dot(basis, right, 0, 0))
    parts = island_parts(right)
    scale2 = whiten(gram)
    left = dot(dot(dot(image, scale, 1, 0), scale2, 1, 0), scale2, 1, 1)
    full = jnp.zeros((islands, width, rank), jnp.float32)
    for s in range(islands):
        full = lax.dynamic_update_slice_in_dim(full, parts[s][None], (me - s) % islands, 0)
    full = full.reshape(cols, rank)
    approx_full = dot(left, full, 1, 1) * (1.0 / islands)
    approx = lax.dynamic_slice_in_dim(approx_full, me * quarter, quarter, 0)
    new_error = (wide - approx_full).astype(jnp.bfloat16)[None]
    new_momentum = momentum_coef * momentum + approx
    new_params = params - outer_rate * (approx + momentum_coef * new_momentum)
    return (new_error, new_params, new_momentum)


def solution(mesh):
    fine = Mesh(mesh.devices.reshape(4, 4, 8, 2), ("x", "y", "z", "c"))
    block = P("x", ROW, None)
    state = P(ROW + ("x",), None)
    return jax.shard_map(
        shards,
        mesh=fine,
        in_specs=(block, block, P(), state, state),
        out_specs=(block, state, state),
        check_vma=False,
    )
```

```python
import jax
import jax.numpy as jnp
from jax import lax
from jax.experimental import pallas as pl
from jax.experimental.pallas import tpu as pltpu
from jax.sharding import Mesh, PartitionSpec as P

ITERS = 4
momentum_coef = 0.9
outer_rate = 0.7
ROW = ("y", "z", "c")


def dot(a, b, ca, cb):
    return lax.dot_general(
        a,
        b,
        (((ca,), (cb,)), ((), ())),
        precision=lax.Precision.HIGHEST,
        preferred_element_type=jnp.float32,
    )


def ring(n, step):
    return [(i, (i + step) % n) for i in range(n)]


def island_parts(v):
    return [v] + [lax.ppermute(v, "x", ring(4, s)) for s in (1, 2, 3)]


def island_sum(v):
    a, b, c, d = island_parts(v)
    return (a + c) + (b + d)


def inverse_factor(gram):
    factor = jnp.linalg.cholesky(gram, symmetrize_input=False)
    eye = jnp.eye(gram.shape[0], dtype=gram.dtype)
    return lax.linalg.triangular_solve(factor, eye, left_side=True, lower=True)


def tiles(v):
    r, w = v.shape
    return v.reshape(r // 8, 8, w // 128, 128).transpose(0, 2, 1, 3).reshape(-1, 8, 128)


def untile(v, r, w):
    return v.reshape(r // 8, w // 128, 8, 128).transpose(0, 2, 1, 3).reshape(r, w)


def row_sum(v):
    parts = tiles(v)
    own = jnp.sum(lax.all_to_all(parts, ROW, 0, 0), axis=0)
    full = lax.all_to_all(jnp.broadcast_to(own, parts.shape), ROW, 0, 0)
    return untile(full, *v.shape)


def combine_kernel(index_ref, grad_ref, buffer_ref, out_ref):
    both = grad_ref[...].astype(jnp.float32) + buffer_ref[...].astype(jnp.float32)
    out_ref[...] = both.astype(jnp.bfloat16).astype(jnp.float32)


def combine_block(index, grad, buffer, width):
    rows = grad.shape[0]
    spec = pl.BlockSpec((rows, width), lambda g, i: (0, i[0]))
    return pl.pallas_call(
        combine_kernel,
        out_shape=jax.ShapeDtypeStruct((rows, width), jnp.float32),
        grid_spec=pltpu.PrefetchScalarGridSpec(
            num_scalar_prefetch=1,
            grid=(1,),
            in_specs=[spec, spec],
            out_specs=pl.BlockSpec((rows, width), lambda g, i: (0, 0)),
        ),
        cost_estimate=pl.CostEstimate(
            flops=rows * width, bytes_accessed=rows * width * 8, transcendentals=0
        ),
        name="combine",
    )(index.reshape(1), grad, buffer)


def finish_kernel(me_ref, left_ref, *refs):
    right_refs, rest = refs[:4], refs[4:]
    grad_ref, buffer_ref, params_ref, momentum_ref = rest[:4]
    error_out, params_out, momentum_out, right, approx = rest[4:]
    step = pl.program_id(0)
    for s in range(4):

        @pl.when(step == s)
        def _(s=s):
            right[...] = right_refs[s][...]

    approx[...] = dot(left_ref[...], right[...], 1, 0)
    both = grad_ref[...].astype(jnp.float32) + buffer_ref[...].astype(jnp.float32)
    combined = both.astype(jnp.bfloat16).astype(jnp.float32)
    error_out[...] = (combined - approx[...]).astype(jnp.bfloat16)
    quarter = params_ref.shape[0]
    mine = approx[pl.ds(me_ref[0] * quarter, quarter), :]
    moved = momentum_coef * momentum_ref[...] + mine
    momentum_out[...] = moved
    params_out[...] = params_ref[...] - outer_rate * (mine + momentum_coef * moved)


def finish(me, left, rights, grad, buffer, params, momentum):
    rows, cols = grad.shape
    quarter = params.shape[0]
    rank, width = rights[0].shape
    islands = len(rights)

    def block(n):
        return pl.BlockSpec((n, width), lambda s, m: (0, lax.rem(m[0] + islands - s, islands)))

    def whole(a):
        return pl.BlockSpec(a.shape, lambda s, m: (0, 0))

    state = jax.ShapeDtypeStruct(params.shape, jnp.float32)
    return pl.pallas_call(
        finish_kernel,
        out_shape=(jax.ShapeDtypeStruct(grad.shape, jnp.bfloat16), state, state),
        grid_spec=pltpu.PrefetchScalarGridSpec(
            num_scalar_prefetch=1,
            grid=(islands,),
            in_specs=[whole(left)]
            + [whole(r) for r in rights]
            + [block(rows), block(rows), block(quarter), block(quarter)],
            out_specs=(block(rows), block(quarter), block(quarter)),
            scratch_shapes=[
                pltpu.VMEM((rank, width), jnp.float32),
                pltpu.VMEM((rows, width), jnp.float32),
            ],
        ),
        name="finish",
    )(me.reshape(1), left, *rights, grad, buffer, params, momentum)


def shards(pseudo_grad, error_buffer, basis_init, params, momentum):
    grad, buffer = pseudo_grad[0], error_buffer[0]
    rows, cols = grad.shape
    rank = basis_init.shape[1]
    islands = lax.axis_size("x")
    me = lax.axis_index("x")
    width = cols // islands

    blocks = {
        s: combine_block(lax.rem(me + s, islands), grad, buffer, width) for s in (2, 1, 3, 0)
    }
    got = {s: lax.ppermute(blocks[s], "x", ring(islands, s)) for s in (2, 1, 3)}
    total = (blocks[0] + got[2]) + (got[1] + got[3])

    both = grad.astype(jnp.float32) + buffer.astype(jnp.float32)
    combined = lax.reduce_precision(both, exponent_bits=8, mantissa_bits=7)
    image = island_sum(dot(basis_init, combined, 0, 1))
    basis = lax.dynamic_slice_in_dim(basis_init, me * width, width, 0).T
    right = row_sum(dot(image, total, 1, 0))
    for sweep in range(1, ITERS):
        part = jnp.concatenate([dot(right, total, 1, 1), dot(basis, right, 1, 1)], axis=1)
        summed = island_sum(part)
        image, gram = summed[:, :rows], summed[:, rows:]
        raw = dot(image, total, 1, 0)
        inverse = inverse_factor(gram)
        basis = dot(inverse, right, 1, 0)
        right = dot(inverse, row_sum(raw), 1, 0)
    gram = island_sum(dot(basis, right, 1, 1))
    rights = island_parts(right)
    last = inverse_factor(gram)
    sketch = dot(last, dot(inverse, image, 1, 0), 1, 0)
    left = dot(sketch, last, 0, 0) * (1.0 / islands)
    new_error, new_params, new_momentum = finish(
        me, left, rights, grad, buffer, params, momentum
    )
    return (new_error[None], new_params, new_momentum)


def solution(mesh):
    fine = Mesh(mesh.devices.reshape(4, 4, 8, 2), ("x", "y", "z", "c"))
    block = P("x", ROW, None)
    state = P(ROW + ("x",), None)
    return jax.shard_map(
        shards,
        mesh=fine,
        in_specs=(block, block, P(), state, state),
        out_specs=(block, state, state),
        check_vma=False,
    )
```

```python
import jax
import jax.numpy as jnp
from jax import lax
from jax.experimental import pallas as pl
from jax.experimental.pallas import tpu as pltpu
from jax.sharding import Mesh, PartitionSpec as P

ITERS = 4
momentum_coef = 0.9
outer_rate = 0.7
ROW = ("y", "z")


def dot(a, b, ca, cb):
    return lax.dot_general(
        a,
        b,
        (((ca,), (cb,)), ((), ())),
        precision=lax.Precision.HIGHEST,
        preferred_element_type=jnp.float32,
    )


def ring(n, step):
    return [(i, (i + step) % n) for i in range(n)]


def island_parts(v):
    return [v] + [lax.ppermute(v, "x", ring(4, s)) for s in (1, 2, 3)]


def island_sum(v):
    a, b, c, d = island_parts(v)
    return (a + c) + (b + d)


def inverse_factor(gram):
    factor = jnp.linalg.cholesky(gram, symmetrize_input=False)
    eye = jnp.eye(gram.shape[0], dtype=gram.dtype)
    return lax.linalg.triangular_solve(factor, eye, left_side=True, lower=True)


def tiles(v):
    r, w = v.shape
    return v.reshape(r // 8, 8, w // 128, 128).transpose(0, 2, 1, 3).reshape(-1, 8, 128)


def untile(v, r, w):
    return v.reshape(r // 8, w // 128, 8, 128).transpose(0, 2, 1, 3).reshape(r, w)


def swap(v):
    return lax.ppermute(v, "c", ring(2, 1))


def row_sum(near, far):
    near = near + swap(far)
    parts = tiles(near)
    own = jnp.sum(lax.all_to_all(parts, ROW, 0, 0), axis=0)
    full = lax.all_to_all(jnp.broadcast_to(own, parts.shape), ROW, 0, 0)
    near = untile(full, *near.shape)
    return jnp.concatenate([near, swap(near)], axis=1)


def combine_kernel(island_ref, core_ref, grad_ref, buffer_ref, top_ref, bottom_ref):
    both = grad_ref[...].astype(jnp.float32) + buffer_ref[...].astype(jnp.float32)
    combined = both.astype(jnp.bfloat16).astype(jnp.float32)
    split = top_ref.shape[0]
    top_ref[...] = combined[:split]
    bottom_ref[...] = combined[split:]


def combine_block(island, core, grad, buffer, width):
    rows = grad.shape[0]
    half = width // 2
    spec = pl.BlockSpec((rows, half), lambda h, i, c: (0, 2 * i[0] + lax.rem(c[0] + h, 2)))
    piece = pl.BlockSpec((rows // 2, half), lambda h, i, c: (0, h))
    shape = jax.ShapeDtypeStruct((rows // 2, width), jnp.float32)
    return pl.pallas_call(
        combine_kernel,
        out_shape=(shape, shape),
        grid_spec=pltpu.PrefetchScalarGridSpec(
            num_scalar_prefetch=2,
            grid=(2,),
            in_specs=[spec, spec],
            out_specs=(piece, piece),
        ),
        cost_estimate=pl.CostEstimate(
            flops=rows * width, bytes_accessed=rows * width * 8, transcendentals=0
        ),
        name="combine",
    )(island.reshape(1), core.reshape(1), grad, buffer)


def low_high(v):
    high = v.astype(jnp.bfloat16)
    return high, (v - high.astype(jnp.float32)).astype(jnp.bfloat16)


def finish_kernel(me_ref, core_ref, left_ref, *refs):
    right_refs, rest = refs[:4], refs[4:]
    grad_ref, buffer_ref, params_ref, momentum_ref = rest[:4]
    error_out, params_out, momentum_out, left4, right, approx = rest[4:]
    step = pl.program_id(0)
    half = grad_ref.shape[1]

    @pl.when(step == 0)
    def _():
        high, low = low_high(left_ref[...])
        left4[...] = jnp.concatenate([high, high, low, low], axis=1)

    for s in range(4):
        for h in range(2):

            @pl.when(step == 2 * s + h)
            def _(s=s, h=h):
                right[...] = right_refs[s][:, h * half : (h + 1) * half]

    high, low = low_high(right[...])
    approx[...] = jnp.dot(
        left4[...],
        jnp.concatenate([high, low, high, low], axis=0),
        preferred_element_type=jnp.float32,
    )
    both = grad_ref[...].astype(jnp.float32) + buffer_ref[...].astype(jnp.float32)
    combined = both.astype(jnp.bfloat16).astype(jnp.float32)
    error_out[...] = (combined - approx[...]).astype(jnp.bfloat16)
    quarter = params_ref.shape[0]
    mine = approx[pl.ds(me_ref[0] * quarter, quarter), :]
    moved = momentum_coef * momentum_ref[...] + mine
    momentum_out[...] = moved
    params_out[...] = params_ref[...] - outer_rate * (mine + momentum_coef * moved)


def finish(me, core, left, rights, grad, buffer, params, momentum):
    rows, cols = grad.shape
    quarter = params.shape[0]
    rank, width = rights[0].shape
    half = width // 2
    islands = len(rights)

    def place(s, m, c):
        island = lax.rem(m[0] + islands - lax.div(s, 2), islands)
        return (0, 2 * island + lax.rem(c[0] + s, 2))

    def block(n):
        return pl.BlockSpec((n, half), place)

    def whole(a):
        return pl.BlockSpec(a.shape, lambda s, m, c: (0, 0))

    state = jax.ShapeDtypeStruct(params.shape, jnp.float32)
    return pl.pallas_call(
        finish_kernel,
        out_shape=(jax.ShapeDtypeStruct(grad.shape, jnp.bfloat16), state, state),
        grid_spec=pltpu.PrefetchScalarGridSpec(
            num_scalar_prefetch=2,
            grid=(2 * islands,),
            in_specs=[whole(left)]
            + [whole(r) for r in rights]
            + [block(rows), block(rows), block(quarter), block(quarter)],
            out_specs=(block(rows), block(quarter), block(quarter)),
            scratch_shapes=[
                pltpu.VMEM((rows, 4 * rank), jnp.bfloat16),
                pltpu.VMEM((rank, half), jnp.float32),
                pltpu.VMEM((rows, half), jnp.float32),
            ],
        ),
        name="finish",
    )(me.reshape(1), core.reshape(1), left, *rights, grad, buffer, params, momentum)


def start_sketch(basis, combined):
    rank = basis.shape[1]
    rest, pieces = basis, []
    for _ in range(3):
        piece = lax.reduce_precision(rest, exponent_bits=8, mantissa_bits=7)
        pieces.append(piece.astype(jnp.bfloat16))
        rest = rest - piece
    wide = lax.dot_general(
        jnp.concatenate(pieces, axis=1),
        combined.astype(jnp.bfloat16),
        (((0,), (1,)), ((), ())),
        preferred_element_type=jnp.float32,
    )
    return wide[2 * rank :] + wide[rank : 2 * rank] + wide[:rank]


def shards(pseudo_grad, error_buffer, basis_init, params, momentum):
    grad, buffer = pseudo_grad[0], error_buffer[0]
    rows, cols = grad.shape
    rank = basis_init.shape[1]
    islands = lax.axis_size("x")
    me = lax.axis_index("x")
    core = lax.axis_index("c")
    width = cols // islands
    half = width // 2

    blocks = {
        s: combine_block(lax.rem(me + s, islands), core, grad, buffer, width)
        for s in (2, 1, 3, 0)
    }
    up, down = ring(islands, 1), ring(islands, -1)
    relay_up = lax.ppermute(blocks[2][0], "x", up)
    relay_down = lax.ppermute(blocks[2][1], "x", down)
    from_below = lax.ppermute(blocks[1][1], "x", up)
    from_above = lax.ppermute(blocks[3][0], "x", down)
    top_below = lax.ppermute(blocks[1][0] + relay_up, "x", up)
    bottom_above = lax.ppermute(blocks[3][1] + relay_down, "x", down)
    total = jnp.concatenate(
        [
            (blocks[0][0] + from_above) + top_below,
            (blocks[0][1] + from_below) + bottom_above,
        ],
        axis=0,
    )

    both = grad.astype(jnp.float32) + buffer.astype(jnp.float32)
    combined = lax.reduce_precision(both, exponent_bits=8, mantissa_bits=7)
    image = island_sum(start_sketch(basis_init, combined))
    basis = lax.dynamic_slice_in_dim(basis_init, me * width, width, 0)
    basis = jnp.where(core == 0, basis, jnp.roll(basis, half, axis=0)).T
    near, far = total[:, :half], total[:, half:]
    right = row_sum(dot(image, near, 1, 0), dot(image, far, 1, 0))
    for sweep in range(1, ITERS):
        part = jnp.concatenate([dot(right, total, 1, 1), dot(basis, right, 1, 1)], axis=1)
        summed = island_sum(part)
        image, gram = summed[:, :rows], summed[:, rows:]
        raw = dot(image, near, 1, 0), dot(image, far, 1, 0)
        inverse = inverse_factor(gram)
        basis = dot(inverse, right, 1, 0)
        right = dot(inverse, row_sum(*raw), 1, 0)
    gram = island_sum(dot(basis, right, 1, 1))
    rights = island_parts(right)
    last = inverse_factor(gram)
    sketch = dot(last, dot(inverse, image, 1, 0), 1, 0)
    left = dot(sketch, last, 0, 0) * (1.0 / islands)
    new_error, new_params, new_momentum = finish(
        me, core, left, rights, grad, buffer, params, momentum
    )
    return (new_error[None], new_params, new_momentum)


def solution(mesh):
    fine = Mesh(mesh.devices.reshape(4, 4, 8, 2), ("x", "y", "z", "c"))
    block = P("x", ROW + ("c",), None)
    state = P(ROW + ("c", "x"), None)
    return jax.shard_map(
        shards,
        mesh=fine,
        in_specs=(block, block, P(), state, state),
        out_specs=(block, state, state),
        check_vma=False,
    )
```

```python
import jax
import jax.numpy as jnp
from jax import lax
from jax.experimental import pallas as pl
from jax.experimental.pallas import tpu as pltpu
from jax.sharding import Mesh, PartitionSpec as P

ITERS = 4
STEP = 4
momentum_coef = 0.9
outer_rate = 0.7
ROW = ("y", "z")


def dot(a, b, ca, cb):
    return lax.dot_general(
        a,
        b,
        (((ca,), (cb,)), ((), ())),
        precision=lax.Precision.HIGHEST,
        preferred_element_type=jnp.float32,
    )


def ring(n, step):
    return [(i, (i + step) % n) for i in range(n)]


def island_parts(v):
    return [v] + [lax.ppermute(v, "x", ring(4, s)) for s in (1, 2, 3)]


def island_sum(v):
    a, b, c, d = island_parts(v)
    return (a + c) + (b + d)


def factor_kernel(gram_ref, out_ref, work):
    n = gram_ref.shape[0]
    lane = lax.broadcasted_iota(jnp.int32, (n, 2 * n), 1)
    row_of = lax.broadcasted_iota(jnp.int32, (n, 2 * n), 0)
    work[:, :n] = gram_ref[...]
    work[:, n:] = jnp.where(lane[:, :n] == row_of[:, :n], 1.0, 0.0)
    below, across = row_of[:, :1], lane[:1]

    def pick(v, lanes, at):
        return jnp.sum(jnp.where(lanes == at, v, 0.0), axis=1, keepdims=True)

    def eliminate(step, carry):
        first = STEP * step
        state = work[...]
        rows = [work[pl.ds(first + i, 1), :] for i in range(STEP)]
        cols = [pick(state, lane, first + i) for i in range(STEP)]
        block = {
            (i, k): pick(rows[i], across, first + k) for i in range(STEP) for k in range(i, STEP)
        }
        for i in range(STEP):
            scale = 1.0 / block[i, i]
            for k in range(i + 1, STEP):
                ratio = block[i, k] * scale
                rows[k] = rows[k] - ratio * rows[i]
                cols[k] = cols[k] - ratio * cols[i]
                for m in range(k, STEP):
                    block[k, m] = block[k, m] - ratio * block[i, m]
            weight = jnp.where(below > first + i, cols[i] * scale, 0.0)
            state = state - weight * rows[i]
        work[...] = state
        return carry

    lax.fori_loop(0, n // STEP, eliminate, 0)
    state = work[...]
    pivots = jnp.sum(jnp.where(lane == row_of, state, 0.0), axis=1, keepdims=True)
    out_ref[...] = state[:, n:] * lax.rsqrt(pivots)


def inverse_factor(gram):
    n = gram.shape[0]
    return pl.pallas_call(
        factor_kernel,
        out_shape=jax.ShapeDtypeStruct((n, n), jnp.float32),
        scratch_shapes=[pltpu.VMEM((n, 2 * n), jnp.float32)],
        cost_estimate=pl.CostEstimate(
            flops=16 * 1024 * 1024, bytes_accessed=16 * 1024 * 1024, transcendentals=0
        ),
        name="factor",
    )(gram)


def tiles(v):
    r, w = v.shape
    return v.reshape(r // 8, 8, w // 128, 128).transpose(0, 2, 1, 3).reshape(-1, 8, 128)


def untile(v, r, w):
    return v.reshape(r // 8, w // 128, 8, 128).transpose(0, 2, 1, 3).reshape(r, w)


def swap(v):
    return lax.ppermute(v, "c", ring(2, 1))


def row_sum(near, far, inverse=None):
    near = near + swap(far)
    parts = tiles(near)
    own = jnp.sum(lax.all_to_all(parts, ROW, 0, 0), axis=0)
    full = lax.all_to_all(jnp.broadcast_to(own, parts.shape), ROW, 0, 0)
    near = untile(full, *near.shape)
    if inverse is not None:
        near = dot(inverse, near, 1, 0)
    return jnp.concatenate([near, swap(near)], axis=1)


def combine_kernel(island_ref, core_ref, grad_ref, buffer_ref, top_ref, bottom_ref):
    both = grad_ref[...].astype(jnp.float32) + buffer_ref[...].astype(jnp.float32)
    combined = both.astype(jnp.bfloat16).astype(jnp.float32)
    split = top_ref.shape[0]
    top_ref[...] = combined[:split]
    bottom_ref[...] = combined[split:]


def combine_block(island, core, grad, buffer, width):
    rows = grad.shape[0]
    half = width // 2
    spec = pl.BlockSpec((rows, half), lambda h, i, c: (0, 2 * i[0] + lax.rem(c[0] + h, 2)))
    piece = pl.BlockSpec((rows // 2, half), lambda h, i, c: (0, h))
    shape = jax.ShapeDtypeStruct((rows // 2, width), jnp.float32)
    return pl.pallas_call(
        combine_kernel,
        out_shape=(shape, shape),
        grid_spec=pltpu.PrefetchScalarGridSpec(
            num_scalar_prefetch=2,
            grid=(2,),
            in_specs=[spec, spec],
            out_specs=(piece, piece),
        ),
        cost_estimate=pl.CostEstimate(
            flops=rows * width, bytes_accessed=rows * width * 8, transcendentals=0
        ),
        name="combine",
    )(island.reshape(1), core.reshape(1), grad, buffer)


def low_high(v):
    high = v.astype(jnp.bfloat16)
    return high, (v - high.astype(jnp.float32)).astype(jnp.bfloat16)


def finish_kernel(me_ref, core_ref, left_ref, *refs):
    right_refs, rest = refs[:4], refs[4:]
    grad_ref, buffer_ref, params_ref, momentum_ref = rest[:4]
    error_out, params_out, momentum_out, left4, mine4, right = rest[4:]
    step = pl.program_id(0)
    half = right.shape[1] // 2
    quarter = params_ref.shape[0]

    @pl.when(step == 0)
    def _():
        high, low = low_high(left_ref[...])
        left4[...] = jnp.concatenate([high, high, low, low], axis=1)
        own = pl.ds(pl.multiple_of(me_ref[0] * quarter, 8), quarter)
        high, low = low_high(left_ref[own, :])
        mine4[...] = jnp.concatenate([high, high, low, low], axis=1)

    near = pl.multiple_of(core_ref[0] * half, half)
    far = pl.multiple_of((1 - core_ref[0]) * half, half)
    for s in range(4):

        @pl.when(step == s)
        def _(s=s):
            right[:, :half] = right_refs[s][:, pl.ds(near, half)]
            right[:, half:] = right_refs[s][:, pl.ds(far, half)]

    high, low = low_high(right[...])
    right4 = jnp.concatenate([high, low, high, low], axis=0)
    approx = jnp.dot(left4[...], right4, preferred_element_type=jnp.float32)
    both = grad_ref[...].astype(jnp.float32) + buffer_ref[...].astype(jnp.float32)
    combined = both.astype(jnp.bfloat16).astype(jnp.float32)
    error_out[...] = (combined - approx).astype(jnp.bfloat16)
    mine = jnp.dot(mine4[...], right4, preferred_element_type=jnp.float32)
    moved = momentum_coef * momentum_ref[...] + mine
    momentum_out[...] = moved
    params_out[...] = params_ref[...] - outer_rate * (mine + momentum_coef * moved)


def finish(me, core, left, rights, grad, buffer, params, momentum):
    rows, _ = grad.shape
    quarter = params.shape[0]
    rank, width = rights[0].shape
    islands = len(rights)

    def block(n):
        return pl.BlockSpec((n, width), lambda s, m, c: (0, lax.rem(m[0] + islands - s, islands)))

    def whole(a):
        return pl.BlockSpec(a.shape, lambda s, m, c: (0, 0))

    state = jax.ShapeDtypeStruct(params.shape, jnp.float32)
    return pl.pallas_call(
        finish_kernel,
        out_shape=(jax.ShapeDtypeStruct(grad.shape, jnp.bfloat16), state, state),
        grid_spec=pltpu.PrefetchScalarGridSpec(
            num_scalar_prefetch=2,
            grid=(islands,),
            in_specs=[whole(left)]
            + [whole(r) for r in rights]
            + [block(rows), block(rows), block(quarter), block(quarter)],
            out_specs=(block(rows), block(quarter), block(quarter)),
            scratch_shapes=[
                pltpu.VMEM((rows, 4 * rank), jnp.bfloat16),
                pltpu.VMEM((quarter, 4 * rank), jnp.bfloat16),
                pltpu.VMEM((rank, width), jnp.float32),
            ],
        ),
        name="finish",
    )(me.reshape(1), core.reshape(1), left, *rights, grad, buffer, params, momentum)


def start_sketch(basis, combined):
    rank = basis.shape[1]
    rest, pieces = basis, []
    for _ in range(3):
        piece = lax.reduce_precision(rest, exponent_bits=8, mantissa_bits=7)
        pieces.append(piece.astype(jnp.bfloat16))
        rest = rest - piece
    wide = lax.dot_general(
        jnp.concatenate(pieces, axis=1),
        combined.astype(jnp.bfloat16),
        (((0,), (1,)), ((), ())),
        preferred_element_type=jnp.float32,
    )
    return wide[2 * rank :] + wide[rank : 2 * rank] + wide[:rank]


def hop(v, pairs):
    return lax.ppermute(v, "x", pairs)


def shards(pseudo_grad, error_buffer, basis_init, params, momentum):
    grad, buffer = pseudo_grad[0], error_buffer[0]
    rows, cols = grad.shape
    islands = lax.axis_size("x")
    me = lax.axis_index("x")
    core = lax.axis_index("c")
    width = cols // islands
    half = width // 2

    blocks = {
        s: combine_block(lax.rem(me + s, islands), core, grad, buffer, width)
        for s in (2, 1, 3, 0)
    }
    up, down = ring(islands, 1), ring(islands, -1)
    relay_up = hop(blocks[2][0], up)
    relay_down = hop(blocks[2][1], down)
    from_below = hop(blocks[1][1], up)
    from_above = hop(blocks[3][0], down)
    top_below = hop(blocks[1][0] + relay_up, up)
    bottom_above = hop(blocks[3][1] + relay_down, down)
    total = jnp.concatenate(
        [
            (blocks[0][0] + from_above) + top_below,
            (blocks[0][1] + from_below) + bottom_above,
        ],
        axis=0,
    )

    both = grad.astype(jnp.float32) + buffer.astype(jnp.float32)
    combined = lax.reduce_precision(both, exponent_bits=8, mantissa_bits=7)
    part = start_sketch(basis_init, combined)
    image = island_sum(part)
    basis = lax.dynamic_slice_in_dim(basis_init, me * width, width, 0)
    basis = jnp.where(core == 0, basis, jnp.roll(basis, half, axis=0)).T
    near, far = total[:, :half], total[:, half:]
    right = row_sum(dot(image, near, 1, 0), dot(image, far, 1, 0))
    for _ in range(1, ITERS):
        part = jnp.concatenate([dot(right, total, 1, 1), dot(basis, right, 1, 1)], axis=1)
        summed = island_sum(part)
        image, gram = summed[:, :rows], summed[:, rows:]
        raw = dot(image, near, 1, 0), dot(image, far, 1, 0)
        inverse = inverse_factor(gram)
        basis = dot(inverse, right, 1, 0)
        right = row_sum(*raw, inverse)
    gram = island_sum(dot(basis, right, 1, 1))
    rights = island_parts(right)
    last = inverse_factor(gram)
    sketch = dot(last, dot(inverse, image, 1, 0), 1, 0)
    left = dot(sketch, last, 0, 0) * (1.0 / islands)
    new_error, new_params, new_momentum = finish(
        me, core, left, rights, grad, buffer, params, momentum
    )
    return (new_error[None], new_params, new_momentum)


def solution(mesh):
    fine = Mesh(mesh.devices.reshape(4, 4, 8, 2), ("x", "y", "z", "c"))
    block = P("x", ROW + ("c",), None)
    state = P(ROW + ("c", "x"), None)
    return jax.shard_map(
        shards,
        mesh=fine,
        in_specs=(block, block, P(), state, state),
        out_specs=(block, state, state),
        check_vma=False,
    )
```

```python
import jax
import jax.numpy as jnp
from jax import lax
from jax.experimental import pallas as pl
from jax.experimental.pallas import tpu as pltpu
from jax.sharding import Mesh, PartitionSpec as P

ITERS = 4
STEP = 4
momentum_coef = 0.9
outer_rate = 0.7
ROW = ("y", "z")


def dot(a, b, ca, cb):
    return lax.dot_general(
        a,
        b,
        (((ca,), (cb,)), ((), ())),
        precision=lax.Precision.HIGHEST,
        preferred_element_type=jnp.float32,
    )


def ring(n, step):
    return [(i, (i + step) % n) for i in range(n)]


def island_parts(v):
    return [v] + [lax.ppermute(v, "x", ring(4, s)) for s in (1, 2, 3)]


def island_sum(v):
    a, b, c, d = island_parts(v)
    return (a + c) + (b + d)


def factor_into(gram, work):
    n = gram.shape[0]
    lane = lax.broadcasted_iota(jnp.int32, (n, 2 * n), 1)
    row_of = lax.broadcasted_iota(jnp.int32, (n, 2 * n), 0)
    work[:, :n] = gram
    work[:, n:] = jnp.where(lane[:, :n] == row_of[:, :n], 1.0, 0.0)
    below, across = row_of[:, :1], lane[:1]

    def pick(v, lanes, at):
        return jnp.sum(jnp.where(lanes == at, v, 0.0), axis=1, keepdims=True)

    def eliminate(step, carry):
        first = STEP * step
        state = work[...]
        rows = [work[pl.ds(first + i, 1), :] for i in range(STEP)]
        cols = [pick(state, lane, first + i) for i in range(STEP)]
        block = {
            (i, k): pick(rows[i], across, first + k) for i in range(STEP) for k in range(i, STEP)
        }
        for i in range(STEP):
            scale = 1.0 / block[i, i]
            for k in range(i + 1, STEP):
                ratio = block[i, k] * scale
                rows[k] = rows[k] - ratio * rows[i]
                cols[k] = cols[k] - ratio * cols[i]
                for m in range(k, STEP):
                    block[k, m] = block[k, m] - ratio * block[i, m]
            weight = jnp.where(below > first + i, cols[i] * scale, 0.0)
            state = state - weight * rows[i]
        work[...] = state
        return carry

    lax.fori_loop(0, n // STEP, eliminate, 0)
    state = work[...]
    pivots = jnp.sum(jnp.where(lane == row_of, state, 0.0), axis=1, keepdims=True)
    return state[:, n:] * lax.rsqrt(pivots)


def factor_kernel(gram_ref, out_ref, work):
    out_ref[...] = factor_into(gram_ref[...], work)


def inverse_factor(gram):
    n = gram.shape[0]
    return pl.pallas_call(
        factor_kernel,
        out_shape=jax.ShapeDtypeStruct((n, n), jnp.float32),
        scratch_shapes=[pltpu.VMEM((n, 2 * n), jnp.float32)],
        cost_estimate=pl.CostEstimate(
            flops=16 * 1024 * 1024, bytes_accessed=16 * 1024 * 1024, transcendentals=0
        ),
        name="factor",
    )(gram)


def tiles(v):
    r, w = v.shape
    return v.reshape(r // 8, 8, w // 128, 128).transpose(0, 2, 1, 3).reshape(-1, 8, 128)


def untile(v, r, w):
    return v.reshape(r // 8, w // 128, 8, 128).transpose(0, 2, 1, 3).reshape(r, w)


def swap(v):
    return lax.ppermute(v, "c", ring(2, 1))


def row_sum(near, far):
    near = near + swap(far)
    parts = tiles(near)
    own = jnp.sum(lax.all_to_all(parts, ROW, 0, 0), axis=0)
    full = lax.all_to_all(jnp.broadcast_to(own, parts.shape), ROW, 0, 0)
    return untile(full, *near.shape)


def combine_kernel(island_ref, core_ref, grad_ref, buffer_ref, top_ref, bottom_ref):
    both = grad_ref[...].astype(jnp.float32) + buffer_ref[...].astype(jnp.float32)
    combined = both.astype(jnp.bfloat16).astype(jnp.float32)
    split = top_ref.shape[0]
    top_ref[...] = combined[:split]
    bottom_ref[...] = combined[split:]


def combine_block(island, core, grad, buffer, width):
    rows = grad.shape[0]
    half = width // 2
    spec = pl.BlockSpec((rows, half), lambda h, i, c: (0, 2 * i[0] + lax.rem(c[0] + h, 2)))
    piece = pl.BlockSpec((rows // 2, half), lambda h, i, c: (0, h))
    shape = jax.ShapeDtypeStruct((rows // 2, width), jnp.float32)
    return pl.pallas_call(
        combine_kernel,
        out_shape=(shape, shape),
        grid_spec=pltpu.PrefetchScalarGridSpec(
            num_scalar_prefetch=2,
            grid=(2,),
            in_specs=[spec, spec],
            out_specs=(piece, piece),
        ),
        cost_estimate=pl.CostEstimate(
            flops=rows * width, bytes_accessed=rows * width * 8, transcendentals=0
        ),
        name="combine",
    )(island.reshape(1), core.reshape(1), grad, buffer)


def low_high(v):
    high = v.astype(jnp.bfloat16)
    return high, (v - high.astype(jnp.float32)).astype(jnp.bfloat16)


def finish_kernel(me_ref, core_ref, gram_ref, sketch_ref, combined_ref, *refs):
    near_refs, far_refs, rest = refs[:4], refs[4:8], refs[8:]
    params_ref, momentum_ref, error_out, params_out, momentum_out = rest[:5]
    left4, mine4, right, left, work = rest[5:]
    step = pl.program_id(0)
    width = right.shape[1]
    half = width // 2
    quarter = params_ref.shape[0]
    islands = len(near_refs)

    @pl.when(step == 0)
    def _():
        last = factor_into(gram_ref[...], work)
        left[...] = dot(dot(last, sketch_ref[...], 1, 0), last, 0, 0) * (1.0 / islands)
        high, low = low_high(left[...])
        left4[...] = jnp.concatenate([high, high, low, low], axis=1)
        own = pl.ds(pl.multiple_of(me_ref[0] * quarter, 8), quarter)
        high, low = low_high(left[own, :])
        mine4[...] = jnp.concatenate([high, high, low, low], axis=1)

    near = pl.multiple_of(core_ref[0] * half, half)
    far = pl.multiple_of((1 - core_ref[0]) * half, half)
    for s in range(islands):

        @pl.when(step == s)
        def _(s=s):
            right[:, pl.ds(near, half)] = near_refs[s][...]
            right[:, pl.ds(far, half)] = far_refs[s][...]

    high, low = low_high(right[...])
    right4 = jnp.concatenate([high, low, high, low], axis=0)
    approx = jnp.dot(left4[...], right4, preferred_element_type=jnp.float32)
    island = lax.rem(me_ref[0] + islands - step, islands)
    columns = pl.ds(pl.multiple_of(island * width, width), width)
    combined = combined_ref[:, columns].astype(jnp.float32)
    error_out[...] = (combined - approx).astype(jnp.bfloat16)
    mine = jnp.dot(mine4[...], right4, preferred_element_type=jnp.float32)
    moved = momentum_coef * momentum_ref[...] + mine
    momentum_out[...] = moved
    params_out[...] = params_ref[...] - outer_rate * (mine + momentum_coef * moved)


def finish(me, core, gram, sketch, combined, nears, fars, params, momentum):
    rows, cols = combined.shape
    quarter = params.shape[0]
    rank, half = nears[0].shape
    islands = len(nears)
    width = 2 * half

    def block(n):
        return pl.BlockSpec((n, width), lambda s, m, c: (0, lax.rem(m[0] + islands - s, islands)))

    whole = pl.BlockSpec(memory_space=pltpu.VMEM)
    state = jax.ShapeDtypeStruct(params.shape, jnp.float32)
    return pl.pallas_call(
        finish_kernel,
        out_shape=(jax.ShapeDtypeStruct((rows, cols), jnp.bfloat16), state, state),
        grid_spec=pltpu.PrefetchScalarGridSpec(
            num_scalar_prefetch=2,
            grid=(islands,),
            in_specs=[whole] * (3 + 2 * islands) + [block(quarter), block(quarter)],
            out_specs=(block(rows), block(quarter), block(quarter)),
            scratch_shapes=[
                pltpu.VMEM((rows, 4 * rank), jnp.bfloat16),
                pltpu.VMEM((quarter, 4 * rank), jnp.bfloat16),
                pltpu.VMEM((rank, width), jnp.float32),
                pltpu.VMEM((rows, rank), jnp.float32),
                pltpu.VMEM((rank, 2 * rank), jnp.float32),
            ],
        ),
        name="finish",
    )(me.reshape(1), core.reshape(1), gram, sketch, combined, *nears, *fars, params, momentum)


def start_sketch(basis, combined):
    rank = basis.shape[1]
    rest, pieces = basis, []
    for _ in range(3):
        piece = lax.reduce_precision(rest, exponent_bits=8, mantissa_bits=7)
        pieces.append(piece.astype(jnp.bfloat16))
        rest = rest - piece
    wide = lax.dot_general(
        jnp.concatenate(pieces, axis=1),
        combined,
        (((0,), (1,)), ((), ())),
        preferred_element_type=jnp.float32,
    )
    return wide[2 * rank :] + wide[rank : 2 * rank] + wide[:rank]


def hop(v, pairs):
    return lax.ppermute(v, "x", pairs)


def shards(pseudo_grad, error_buffer, basis_init, params, momentum):
    grad, buffer = pseudo_grad[0], error_buffer[0]
    rows, cols = grad.shape
    rank = basis_init.shape[1]
    islands = lax.axis_size("x")
    me = lax.axis_index("x")
    core = lax.axis_index("c")
    width = cols // islands
    half = width // 2

    blocks = {
        s: combine_block(lax.rem(me + s, islands), core, grad, buffer, width)
        for s in (2, 1, 3, 0)
    }
    up, down = ring(islands, 1), ring(islands, -1)
    relay_up = hop(blocks[2][0], up)
    relay_down = hop(blocks[2][1], down)
    from_below = hop(blocks[1][1], up)
    from_above = hop(blocks[3][0], down)
    top_below = hop(blocks[1][0] + relay_up, up)
    bottom_above = hop(blocks[3][1] + relay_down, down)
    total = jnp.concatenate(
        [
            (blocks[0][0] + from_above) + top_below,
            (blocks[0][1] + from_below) + bottom_above,
        ],
        axis=0,
    )

    both = grad.astype(jnp.float32) + buffer.astype(jnp.float32)
    combined = lax.reduce_precision(both, exponent_bits=8, mantissa_bits=7)
    combined = lax.optimization_barrier(combined.astype(jnp.bfloat16))
    part = start_sketch(basis_init, combined)
    image = island_sum(part)
    basis = lax.dynamic_slice_in_dim(basis_init, me * width, width, 0)
    basis = jnp.where(core == 0, basis, jnp.roll(basis, half, axis=0)).T
    side = rank // 2

    def gram_half(basis, right):
        own = lax.dynamic_slice_in_dim(basis, core * side, side, 0)
        return dot(right, own, 1, 1)

    def gram_whole(own):
        other = swap(own)
        first, second = jnp.where(core == 0, own, other), jnp.where(core == 0, other, own)
        return jnp.concatenate([first, second], axis=1)

    def raw_sum(image):
        return row_sum(dot(image, total[:, :half], 1, 0), dot(image, total[:, half:], 1, 0))

    near = raw_sum(image)

    def sweep(_, carry):
        near, basis = carry[:2]
        far = swap(near)
        right = jnp.concatenate([near, far], axis=1)
        part = jnp.concatenate([dot(right, total, 1, 1), gram_half(basis, right)], axis=1)
        summed = island_sum(part)
        image = summed[:, :rows]
        raw = raw_sum(image)
        inverse = inverse_factor(gram_whole(summed[:, rows:]))
        basis = dot(inverse, right, 1, 0)
        near = dot(inverse, raw, 1, 0)
        return near, basis, image, inverse

    square = jnp.zeros((rank, rank), jnp.float32)
    near, basis, image, inverse = lax.fori_loop(
        1, ITERS, sweep, (near, basis, jnp.zeros_like(image), square)
    )
    nears = island_parts(near)
    far = swap(near)
    others = swap(jnp.stack(nears[1:]))
    fars = [far] + [others[i] for i in range(islands - 1)]
    right = jnp.concatenate([near, fars[0]], axis=1)
    gram = island_sum(dot(basis, right, 1, 1))
    sketch = dot(inverse, image, 1, 0)
    new_error, new_params, new_momentum = finish(
        me, core, gram, sketch, combined, nears, fars, params, momentum
    )
    return (new_error[None], new_params, new_momentum)


def solution(mesh):
    fine = Mesh(mesh.devices.reshape(4, 4, 8, 2), ("x", "y", "z", "c"))
    block = P("x", ROW + ("c",), None)
    state = P(ROW + ("c", "x"), None)
    return jax.shard_map(
        shards,
        mesh=fine,
        in_specs=(block, block, P(), state, state),
        out_specs=(block, state, state),
        check_vma=False,
    )
```

```python
import jax
import jax.numpy as jnp
from jax import lax
from jax.experimental import pallas as pl
from jax.experimental.pallas import tpu as pltpu
from jax.sharding import Mesh, PartitionSpec as P

ITERS = 4
STEP = 4
momentum_coef = 0.9
outer_rate = 0.7
ROW = ("y", "z")


def dot(a, b, ca, cb):
    return lax.dot_general(
        a,
        b,
        (((ca,), (cb,)), ((), ())),
        precision=lax.Precision.HIGHEST,
        preferred_element_type=jnp.float32,
    )


def ring(n, step):
    return [(i, (i + step) % n) for i in range(n)]


def island_parts(v):
    return [v] + [lax.ppermute(v, "x", ring(4, s)) for s in (1, 2, 3)]


def island_sum(v):
    a, b, c, d = island_parts(v)
    return (a + c) + (b + d)


def factor_into(gram, work):
    n = gram.shape[0]
    lane = lax.broadcasted_iota(jnp.int32, (n, 2 * n), 1)
    row_of = lax.broadcasted_iota(jnp.int32, (n, 2 * n), 0)
    work[:, :n] = gram
    work[:, n:] = jnp.where(lane[:, :n] == row_of[:, :n], 1.0, 0.0)
    below, across = row_of[:, :1], lane[:1]

    def pick(v, lanes, at):
        return jnp.sum(jnp.where(lanes == at, v, 0.0), axis=1, keepdims=True)

    def eliminate(step, carry):
        first = STEP * step
        state = work[...]
        rows = [work[pl.ds(first + i, 1), :] for i in range(STEP)]
        cols = [pick(state, lane, first + i) for i in range(STEP)]
        block = {
            (i, k): pick(rows[i], across, first + k) for i in range(STEP) for k in range(i, STEP)
        }
        for i in range(STEP):
            scale = 1.0 / block[i, i]
            for k in range(i + 1, STEP):
                ratio = block[i, k] * scale
                rows[k] = rows[k] - ratio * rows[i]
                cols[k] = cols[k] - ratio * cols[i]
                for m in range(k, STEP):
                    block[k, m] = block[k, m] - ratio * block[i, m]
            weight = jnp.where(below > first + i, cols[i] * scale, 0.0)
            state = state - weight * rows[i]
        work[...] = state
        return carry

    lax.fori_loop(0, n // STEP, eliminate, 0)
    state = work[...]
    pivots = jnp.sum(jnp.where(lane == row_of, state, 0.0), axis=1, keepdims=True)
    return state[:, n:] * lax.rsqrt(pivots)


def factor_kernel(gram_ref, out_ref, work):
    out_ref[...] = factor_into(gram_ref[...], work)


def inverse_factor(gram):
    n = gram.shape[0]
    return pl.pallas_call(
        factor_kernel,
        out_shape=jax.ShapeDtypeStruct((n, n), jnp.float32),
        scratch_shapes=[pltpu.VMEM((n, 2 * n), jnp.float32)],
        cost_estimate=pl.CostEstimate(
            flops=16 * 1024 * 1024, bytes_accessed=16 * 1024 * 1024, transcendentals=0
        ),
        name="factor",
    )(gram)


def tiles(v):
    r, w = v.shape
    return v.reshape(r // 8, 8, w // 128, 128).transpose(0, 2, 1, 3).reshape(-1, 8, 128)


def untile(v, r, w):
    return v.reshape(r // 8, w // 128, 8, 128).transpose(0, 2, 1, 3).reshape(r, w)


def swap(v):
    return lax.ppermute(v, "c", ring(2, 1))


def row_sum(near, far):
    near = near + swap(far)
    parts = tiles(near)
    own = jnp.sum(lax.all_to_all(parts, ROW, 0, 0), axis=0)
    full = lax.all_to_all(jnp.broadcast_to(own, parts.shape), ROW, 0, 0)
    return untile(full, *near.shape)


def combine_kernel(island_ref, core_ref, grad_ref, buffer_ref, top_ref, bottom_ref):
    both = grad_ref[...].astype(jnp.float32) + buffer_ref[...].astype(jnp.float32)
    combined = both.astype(jnp.bfloat16).astype(jnp.float32)
    split = top_ref.shape[0]
    top_ref[...] = combined[:split]
    bottom_ref[...] = combined[split:]


def combine_block(island, core, grad, buffer, width):
    rows = grad.shape[0]
    half = width // 2
    spec = pl.BlockSpec((rows, half), lambda h, i, c: (0, 2 * i[0] + lax.rem(c[0] + h, 2)))
    piece = pl.BlockSpec((rows // 2, half), lambda h, i, c: (0, h))
    shape = jax.ShapeDtypeStruct((rows // 2, width), jnp.float32)
    return pl.pallas_call(
        combine_kernel,
        out_shape=(shape, shape),
        grid_spec=pltpu.PrefetchScalarGridSpec(
            num_scalar_prefetch=2,
            grid=(2,),
            in_specs=[spec, spec],
            out_specs=(piece, piece),
        ),
        cost_estimate=pl.CostEstimate(
            flops=rows * width, bytes_accessed=rows * width * 8, transcendentals=0
        ),
        name="combine",
    )(island.reshape(1), core.reshape(1), grad, buffer)


def low_high(v):
    high = v.astype(jnp.bfloat16)
    return high, (v - high.astype(jnp.float32)).astype(jnp.bfloat16)


def finish_kernel(me_ref, core_ref, *refs):
    gram_refs, near_refs, refs = refs[:4], refs[4:8], refs[8:]
    far_ref, others_ref, inverse_ref, image_ref, combined_ref = refs[:5]
    far_refs = [far_ref] + [others_ref.at[i] for i in range(3)]
    rest = refs[5:]
    params_ref, momentum_ref, error_out, params_out, momentum_out = rest[:5]
    left4, mine4, right, left, work = rest[5:]
    step = pl.program_id(0)
    width = right.shape[1]
    half = width // 2
    quarter = params_ref.shape[0]
    islands = len(near_refs)

    @pl.when(step == 0)
    def _():
        a, b, c, d = [ref[...] for ref in gram_refs]
        last = factor_into((a + c) + (b + d), work)
        sketch = dot(inverse_ref[...], image_ref[...], 1, 0)
        left[...] = dot(dot(last, sketch, 1, 0), last, 0, 0) * (1.0 / islands)
        high, low = low_high(left[...])
        left4[...] = jnp.concatenate([high, high, low, low], axis=1)
        own = pl.ds(pl.multiple_of(me_ref[0] * quarter, 8), quarter)
        high, low = low_high(left[own, :])
        mine4[...] = jnp.concatenate([high, high, low, low], axis=1)

    near = pl.multiple_of(core_ref[0] * half, half)
    far = pl.multiple_of((1 - core_ref[0]) * half, half)
    for s in range(islands):

        @pl.when(step == s)
        def _(s=s):
            right[:, pl.ds(near, half)] = near_refs[s][...]
            right[:, pl.ds(far, half)] = far_refs[s][...]

    high, low = low_high(right[...])
    right4 = jnp.concatenate([high, low, high, low], axis=0)
    approx = jnp.dot(left4[...], right4, preferred_element_type=jnp.float32)
    island = lax.rem(me_ref[0] + islands - step, islands)
    columns = pl.ds(pl.multiple_of(island * width, width), width)
    combined = combined_ref[:, columns].astype(jnp.float32)
    error_out[...] = (combined - approx).astype(jnp.bfloat16)
    mine = jnp.dot(mine4[...], right4, preferred_element_type=jnp.float32)
    moved = momentum_coef * momentum_ref[...] + mine
    momentum_out[...] = moved
    params_out[...] = params_ref[...] - outer_rate * (mine + momentum_coef * moved)


def finish(me, core, grams, nears, far, others, inverse, image, combined, params, momentum):
    rows, cols = combined.shape
    quarter = params.shape[0]
    rank, half = nears[0].shape
    islands = len(nears)
    width = 2 * half

    def block(n):
        return pl.BlockSpec((n, width), lambda s, m, c: (0, lax.rem(m[0] + islands - s, islands)))

    whole = pl.BlockSpec(memory_space=pltpu.VMEM)
    state = jax.ShapeDtypeStruct(params.shape, jnp.float32)
    return pl.pallas_call(
        finish_kernel,
        out_shape=(jax.ShapeDtypeStruct((rows, cols), jnp.bfloat16), state, state),
        grid_spec=pltpu.PrefetchScalarGridSpec(
            num_scalar_prefetch=2,
            grid=(islands,),
            in_specs=[whole] * (5 + 2 * islands) + [block(quarter), block(quarter)],
            out_specs=(block(rows), block(quarter), block(quarter)),
            scratch_shapes=[
                pltpu.VMEM((rows, 4 * rank), jnp.bfloat16),
                pltpu.VMEM((quarter, 4 * rank), jnp.bfloat16),
                pltpu.VMEM((rank, width), jnp.float32),
                pltpu.VMEM((rows, rank), jnp.float32),
                pltpu.VMEM((rank, 2 * rank), jnp.float32),
            ],
        ),
        name="finish",
    )(
        me.reshape(1),
        core.reshape(1),
        *grams,
        *nears,
        far,
        others,
        inverse,
        image,
        combined,
        params,
        momentum,
    )


def start_sketch(basis, combined):
    rank = basis.shape[1]
    rest, pieces = basis, []
    for _ in range(3):
        piece = lax.reduce_precision(rest, exponent_bits=8, mantissa_bits=7)
        pieces.append(piece.astype(jnp.bfloat16))
        rest = rest - piece
    wide = lax.dot_general(
        jnp.concatenate(pieces, axis=1),
        combined,
        (((0,), (1,)), ((), ())),
        preferred_element_type=jnp.float32,
    )
    return wide[2 * rank :] + wide[rank : 2 * rank] + wide[:rank]


def hop(v, pairs):
    return lax.ppermute(v, "x", pairs)


def shards(pseudo_grad, error_buffer, basis_init, params, momentum):
    grad, buffer = pseudo_grad[0], error_buffer[0]
    rows, cols = grad.shape
    rank = basis_init.shape[1]
    islands = lax.axis_size("x")
    me = lax.axis_index("x")
    core = lax.axis_index("c")
    width = cols // islands
    half = width // 2

    blocks = {
        s: combine_block(lax.rem(me + s, islands), core, grad, buffer, width)
        for s in (2, 1, 3, 0)
    }
    up, down = ring(islands, 1), ring(islands, -1)
    relay_up = hop(blocks[2][0], up)
    relay_down = hop(blocks[2][1], down)
    from_below = hop(blocks[1][1], up)
    from_above = hop(blocks[3][0], down)
    top_below = hop(blocks[1][0] + relay_up, up)
    bottom_above = hop(blocks[3][1] + relay_down, down)
    both = grad.astype(jnp.float32) + buffer.astype(jnp.float32)
    combined = lax.reduce_precision(both, exponent_bits=8, mantissa_bits=7)
    combined = lax.optimization_barrier(combined.astype(jnp.bfloat16))
    part = start_sketch(basis_init, combined)
    image = island_sum(part)
    basis = lax.dynamic_slice_in_dim(basis_init, me * width, width, 0)
    basis = jnp.where(core == 0, basis, jnp.roll(basis, half, axis=0)).T
    side = rank // 2
    hold = lax.optimization_barrier

    top = hold(blocks[0][0] + from_above)
    bottom = hold(blocks[0][1] + from_below)
    split = top.shape[0]
    early = hold(dot(image[:, :split], top, 1, 0) + dot(image[:, split:], bottom, 1, 0))
    top_image, bottom_image = image[:, :split], image[:, split:]

    def late(columns):
        return (
            early[:, columns]
            + dot(top_image, top_below[:, columns], 1, 0)
            + dot(bottom_image, bottom_above[:, columns], 1, 0)
        )

    near_columns, far_columns = slice(0, half), slice(half, width)
    far_part = late(far_columns)
    near_part = hold(late(near_columns))
    near = row_sum(near_part, far_part)
    total_near, total_far = hold(
        tuple(
            jnp.concatenate(
                [top[:, c] + top_below[:, c], bottom[:, c] + bottom_above[:, c]], axis=0
            )
            for c in (near_columns, far_columns)
        )
    )

    def own_rows(basis):
        return lax.dynamic_slice_in_dim(basis, core * side, side, 0)

    def gram_whole(own):
        other = swap(own)
        first, second = jnp.where(core == 0, own, other), jnp.where(core == 0, other, own)
        return jnp.concatenate([first, second], axis=1)

    def raw_sum(image):
        far_part = dot(image, total_far, 1, 0)
        return row_sum(hold(dot(image, total_near, 1, 0)), far_part)

    def sweep(_, carry):
        near, basis_near, basis_far = carry[:3]
        far = swap(near)
        image = hold(dot(near, total_near, 1, 1))
        gram = hold(dot(near, own_rows(basis_near), 1, 1))
        image = image + dot(far, total_far, 1, 1)
        gram = gram + dot(far, own_rows(basis_far), 1, 1)
        summed = island_sum(jnp.concatenate([image, gram], axis=1))
        image = summed[:, :rows]
        raw = raw_sum(image)
        inverse = inverse_factor(gram_whole(summed[:, rows:]))
        basis_near = dot(inverse, near, 1, 0)
        basis_far = dot(inverse, far, 1, 0)
        near = dot(inverse, raw, 1, 0)
        return near, basis_near, basis_far, image, inverse

    square = jnp.zeros((rank, rank), jnp.float32)
    near, basis_near, basis_far, image, inverse = lax.fori_loop(
        1,
        ITERS,
        sweep,
        (near, basis[:, :half], basis[:, half:], jnp.zeros_like(image), square),
    )
    nears = island_parts(near)
    far = swap(near)
    gram = hold(dot(basis_near, near, 1, 1)) + dot(basis_far, far, 1, 1)
    grams = island_parts(gram)
    stacked = jnp.stack(nears[1:])
    others = swap(stacked)
    new_error, new_params, new_momentum = finish(
        me,
        core,
        grams,
        nears,
        far,
        others,
        inverse,
        image,
        combined,
        params,
        momentum,
    )
    return (new_error[None], new_params, new_momentum)


def solution(mesh):
    fine = Mesh(mesh.devices.reshape(4, 4, 8, 2), ("x", "y", "z", "c"))
    block = P("x", ROW + ("c",), None)
    state = P(ROW + ("c", "x"), None)
    return jax.shard_map(
        shards,
        mesh=fine,
        in_specs=(block, block, P(), state, state),
        out_specs=(block, state, state),
        check_vma=False,
    )
```

```python
import jax
import jax.numpy as jnp
from jax import lax
from jax.experimental import pallas as pl
from jax.experimental.pallas import tpu as pltpu
from jax.sharding import Mesh, PartitionSpec as P

ITERS = 4
STEP = 4
momentum_coef = 0.9
outer_rate = 0.7
ROW = ("y", "z")


def dot(a, b, ca, cb):
    return lax.dot_general(
        a,
        b,
        (((ca,), (cb,)), ((), ())),
        precision=lax.Precision.HIGHEST,
        preferred_element_type=jnp.float32,
    )


def ring(n, step):
    return [(i, (i + step) % n) for i in range(n)]


def island_parts(v):
    return [v] + [lax.ppermute(v, "x", ring(4, s)) for s in (1, 2, 3)]


def island_sum(v):
    a, b, c, d = island_parts(v)
    return (a + c) + (b + d)


def factor_into(gram, work):
    n = gram.shape[0]
    lane = lax.broadcasted_iota(jnp.int32, (n, 2 * n), 1)
    row_of = lax.broadcasted_iota(jnp.int32, (n, 2 * n), 0)
    work[:, :n] = gram
    work[:, n:] = jnp.where(lane[:, :n] == row_of[:, :n], 1.0, 0.0)
    below, across = row_of[:, :1], lane[:1]

    def pick(v, lanes, at):
        return jnp.sum(jnp.where(lanes == at, v, 0.0), axis=1, keepdims=True)

    def eliminate(step, carry):
        first = STEP * step
        state = work[...]
        rows = [work[pl.ds(first + i, 1), :] for i in range(STEP)]
        cols = [pick(state, lane, first + i) for i in range(STEP)]
        block = {
            (i, k): pick(rows[i], across, first + k) for i in range(STEP) for k in range(i, STEP)
        }
        for i in range(STEP):
            scale = 1.0 / block[i, i]
            for k in range(i + 1, STEP):
                ratio = block[i, k] * scale
                rows[k] = rows[k] - ratio * rows[i]
                cols[k] = cols[k] - ratio * cols[i]
                for m in range(k, STEP):
                    block[k, m] = block[k, m] - ratio * block[i, m]
            weight = jnp.where(below > first + i, cols[i] * scale, 0.0)
            state = state - weight * rows[i]
        work[...] = state
        return carry

    lax.fori_loop(0, n // STEP, eliminate, 0)
    state = work[...]
    pivots = jnp.sum(jnp.where(lane == row_of, state, 0.0), axis=1, keepdims=True)
    return state[:, n:] * lax.rsqrt(pivots)


def factor_kernel(gram_ref, out_ref, work):
    out_ref[...] = factor_into(gram_ref[...], work)


def inverse_factor(gram):
    n = gram.shape[0]
    return pl.pallas_call(
        factor_kernel,
        out_shape=jax.ShapeDtypeStruct((n, n), jnp.float32),
        scratch_shapes=[pltpu.VMEM((n, 2 * n), jnp.float32)],
        cost_estimate=pl.CostEstimate(
            flops=16 * 1024 * 1024, bytes_accessed=16 * 1024 * 1024, transcendentals=0
        ),
        name="factor",
    )(gram)


def tiles(v):
    r, w = v.shape
    return v.reshape(r // 8, 8, w // 128, 128).transpose(0, 2, 1, 3).reshape(-1, 8, 128)


def untile(v, r, w):
    return v.reshape(r // 8, w // 128, 8, 128).transpose(0, 2, 1, 3).reshape(r, w)


def swap(v):
    return lax.ppermute(v, "c", ring(2, 1))


def row_sum(near, far):
    near = near + swap(far)
    parts = tiles(near)
    own = jnp.sum(lax.all_to_all(parts, ROW, 0, 0), axis=0)
    full = lax.all_to_all(jnp.broadcast_to(own, parts.shape), ROW, 0, 0)
    return untile(full, *near.shape)


def combine_kernel(island_ref, core_ref, grad_ref, buffer_ref, top_ref, bottom_ref):
    both = grad_ref[...].astype(jnp.float32) + buffer_ref[...].astype(jnp.float32)
    combined = both.astype(jnp.bfloat16).astype(jnp.float32)
    split = top_ref.shape[0]
    top_ref[...] = combined[:split]
    bottom_ref[...] = combined[split:]


def combine_block(island, core, grad, buffer, width):
    rows = grad.shape[0]
    half = width // 2
    spec = pl.BlockSpec((rows, half), lambda h, i, c: (0, 2 * i[0] + lax.rem(c[0] + h, 2)))
    piece = pl.BlockSpec((rows // 2, half), lambda h, i, c: (0, h))
    shape = jax.ShapeDtypeStruct((rows // 2, width), jnp.float32)
    return pl.pallas_call(
        combine_kernel,
        out_shape=(shape, shape),
        grid_spec=pltpu.PrefetchScalarGridSpec(
            num_scalar_prefetch=2,
            grid=(2,),
            in_specs=[spec, spec],
            out_specs=(piece, piece),
        ),
        cost_estimate=pl.CostEstimate(
            flops=rows * width, bytes_accessed=rows * width * 8, transcendentals=0
        ),
        name="combine",
    )(island.reshape(1), core.reshape(1), grad, buffer)


def low_high(v):
    high = v.astype(jnp.bfloat16)
    return high, (v - high.astype(jnp.float32)).astype(jnp.bfloat16)


def finish_kernel(me_ref, core_ref, *refs):
    gram_refs, near_refs, refs = refs[:4], refs[4:8], refs[8:]
    far_ref, others_ref, inverse_ref, image_ref, combined_ref = refs[:5]
    far_refs = [far_ref] + [others_ref.at[i] for i in range(3)]
    rest = refs[5:]
    params_ref, momentum_ref, error_out, params_out, momentum_out = rest[:5]
    left4, mine4, right, left, work = rest[5:]
    step = pl.program_id(0)
    width = right.shape[1]
    half = width // 2
    quarter = params_ref.shape[0]
    islands = len(near_refs)

    @pl.when(step == 0)
    def _():
        a, b, c, d = [ref[...] for ref in gram_refs]
        last = factor_into((a + c) + (b + d), work)
        sketch = dot(inverse_ref[...], image_ref[...], 1, 0)
        left[...] = dot(dot(last, sketch, 1, 0), last, 0, 0) * (1.0 / islands)
        high, low = low_high(left[...])
        left4[...] = jnp.concatenate([high, high, low, low], axis=1)
        own = pl.ds(pl.multiple_of(me_ref[0] * quarter, 8), quarter)
        high, low = low_high(left[own, :])
        mine4[...] = jnp.concatenate([high, high, low, low], axis=1)

    near = pl.multiple_of(core_ref[0] * half, half)
    far = pl.multiple_of((1 - core_ref[0]) * half, half)
    for s in range(islands):

        @pl.when(step == s)
        def _(s=s):
            right[:, pl.ds(near, half)] = near_refs[s][...]
            right[:, pl.ds(far, half)] = far_refs[s][...]

    high, low = low_high(right[...])
    right4 = jnp.concatenate([high, low, high, low], axis=0)
    approx = jnp.dot(left4[...], right4, preferred_element_type=jnp.float32)
    island = lax.rem(me_ref[0] + islands - step, islands)
    columns = pl.ds(pl.multiple_of(island * width, width), width)
    combined = combined_ref[:, columns].astype(jnp.float32)
    error_out[...] = (combined - approx).astype(jnp.bfloat16)
    mine = jnp.dot(mine4[...], right4, preferred_element_type=jnp.float32)
    moved = momentum_coef * momentum_ref[...] + mine
    momentum_out[...] = moved
    params_out[...] = params_ref[...] - outer_rate * (mine + momentum_coef * moved)


def finish(me, core, grams, nears, far, others, inverse, image, combined, params, momentum):
    rows, cols = combined.shape
    quarter = params.shape[0]
    rank, half = nears[0].shape
    islands = len(nears)
    width = 2 * half

    def block(n):
        return pl.BlockSpec((n, width), lambda s, m, c: (0, lax.rem(m[0] + islands - s, islands)))

    whole = pl.BlockSpec(memory_space=pltpu.VMEM)
    state = jax.ShapeDtypeStruct(params.shape, jnp.float32)
    return pl.pallas_call(
        finish_kernel,
        out_shape=(jax.ShapeDtypeStruct((rows, cols), jnp.bfloat16), state, state),
        grid_spec=pltpu.PrefetchScalarGridSpec(
            num_scalar_prefetch=2,
            grid=(islands,),
            in_specs=[whole] * (5 + 2 * islands) + [block(quarter), block(quarter)],
            out_specs=(block(rows), block(quarter), block(quarter)),
            scratch_shapes=[
                pltpu.VMEM((rows, 4 * rank), jnp.bfloat16),
                pltpu.VMEM((quarter, 4 * rank), jnp.bfloat16),
                pltpu.VMEM((rank, width), jnp.float32),
                pltpu.VMEM((rows, rank), jnp.float32),
                pltpu.VMEM((rank, 2 * rank), jnp.float32),
            ],
        ),
        name="finish",
    )(
        me.reshape(1),
        core.reshape(1),
        *grams,
        *nears,
        far,
        others,
        inverse,
        image,
        combined,
        params,
        momentum,
    )


def split_basis(basis):
    rest, pieces = basis, []
    for _ in range(3):
        piece = lax.reduce_precision(rest, exponent_bits=8, mantissa_bits=7)
        pieces.append(piece.astype(jnp.bfloat16))
        rest = rest - piece
    return jnp.concatenate(pieces, axis=1)


def start_sketch(pieces, combined):
    rank = pieces.shape[1] // 3
    wide = lax.dot_general(
        pieces, combined, (((0,), (1,)), ((), ())), preferred_element_type=jnp.float32
    )
    return wide[2 * rank :] + wide[rank : 2 * rank] + wide[:rank]


def hop(v, pairs):
    return lax.ppermute(v, "x", pairs)


def shards(pseudo_grad, error_buffer, basis_init, params, momentum):
    grad, buffer = pseudo_grad[0], error_buffer[0]
    rows, cols = grad.shape
    rank = basis_init.shape[1]
    islands = lax.axis_size("x")
    me = lax.axis_index("x")
    core = lax.axis_index("c")
    width = cols // islands
    half = width // 2

    blocks = {
        s: combine_block(lax.rem(me + s, islands), core, grad, buffer, width)
        for s in (2, 1, 3, 0)
    }
    up, down = ring(islands, 1), ring(islands, -1)
    relay_up = hop(blocks[2][0], up)
    relay_down = hop(blocks[2][1], down)
    from_below = hop(blocks[1][1], up)
    from_above = hop(blocks[3][0], down)
    both = grad.astype(jnp.float32) + buffer.astype(jnp.float32)
    combined = lax.reduce_precision(both, exponent_bits=8, mantissa_bits=7)
    hold = lax.optimization_barrier
    combined = hold(combined.astype(jnp.bfloat16))
    pieces, up_sum, down_sum = hold(
        (split_basis(basis_init), blocks[1][0] + relay_up, blocks[3][1] + relay_down)
    )
    top_below = hop(up_sum, up)
    bottom_above = hop(down_sum, down)
    part = start_sketch(pieces, combined)
    image = island_sum(part)
    basis = lax.dynamic_slice_in_dim(basis_init, me * width, width, 0)
    basis = jnp.where(core == 0, basis, jnp.roll(basis, half, axis=0)).T
    side = rank // 2

    top = hold(blocks[0][0] + from_above)
    bottom = hold(blocks[0][1] + from_below)
    split = top.shape[0]
    early = hold(dot(image[:, :split], top, 1, 0) + dot(image[:, split:], bottom, 1, 0))
    top_image, bottom_image = image[:, :split], image[:, split:]

    def late(columns):
        return (
            early[:, columns]
            + dot(top_image, top_below[:, columns], 1, 0)
            + dot(bottom_image, bottom_above[:, columns], 1, 0)
        )

    near_columns, far_columns = slice(0, half), slice(half, width)
    far_part = late(far_columns)
    near_part = hold(late(near_columns))
    near = row_sum(near_part, far_part)
    total_near, total_far = hold(
        tuple(
            jnp.concatenate(
                [top[:, c] + top_below[:, c], bottom[:, c] + bottom_above[:, c]], axis=0
            )
            for c in (near_columns, far_columns)
        )
    )

    def own_rows(basis):
        return lax.dynamic_slice_in_dim(basis, core * side, side, 0)

    def gram_whole(own):
        other = swap(own)
        first, second = jnp.where(core == 0, own, other), jnp.where(core == 0, other, own)
        return jnp.concatenate([first, second], axis=1)

    def raw_sum(image):
        far_part = dot(image, total_far, 1, 0)
        return row_sum(hold(dot(image, total_near, 1, 0)), far_part)

    def sweep(_, carry):
        near, basis_near, basis_far = carry[:3]
        far = swap(near)
        image = hold(dot(near, total_near, 1, 1))
        gram = hold(dot(near, own_rows(basis_near), 1, 1))
        image = image + dot(far, total_far, 1, 1)
        gram = gram + dot(far, own_rows(basis_far), 1, 1)
        summed = island_sum(jnp.concatenate([image, gram], axis=1))
        image = summed[:, :rows]
        raw = raw_sum(image)
        inverse = inverse_factor(gram_whole(summed[:, rows:]))
        basis_near = dot(inverse, near, 1, 0)
        basis_far = dot(inverse, far, 1, 0)
        near = dot(inverse, raw, 1, 0)
        return near, basis_near, basis_far, image, inverse

    square = jnp.zeros((rank, rank), jnp.float32)
    near, basis_near, basis_far, image, inverse = lax.fori_loop(
        1,
        ITERS,
        sweep,
        (near, basis[:, :half], basis[:, half:], jnp.zeros_like(image), square),
    )
    nears = island_parts(near)
    far = swap(near)
    gram = hold(dot(basis_near, near, 1, 1)) + dot(basis_far, far, 1, 1)
    grams = island_parts(gram)
    stacked = jnp.stack(nears[1:])
    others = swap(stacked)
    new_error, new_params, new_momentum = finish(
        me,
        core,
        grams,
        nears,
        far,
        others,
        inverse,
        image,
        combined,
        params,
        momentum,
    )
    return (new_error[None], new_params, new_momentum)


def solution(mesh):
    fine = Mesh(mesh.devices.reshape(4, 4, 8, 2), ("x", "y", "z", "c"))
    block = P("x", ROW + ("c",), None)
    state = P(ROW + ("c", "x"), None)
    return jax.shard_map(
        shards,
        mesh=fine,
        in_specs=(block, block, P(), state, state),
        out_specs=(block, state, state),
        check_vma=False,
    )
```

```python
import jax
import jax.numpy as jnp
from jax import lax
from jax.experimental import pallas as pl
from jax.experimental.pallas import tpu as pltpu
from jax.sharding import Mesh, PartitionSpec as P

ITERS = 4
STEP = 4
momentum_coef = 0.9
outer_rate = 0.7
ROW = ("y", "z")


def dot(a, b, ca, cb):
    return lax.dot_general(
        a,
        b,
        (((ca,), (cb,)), ((), ())),
        precision=lax.Precision.HIGHEST,
        preferred_element_type=jnp.float32,
    )


def ring(n, step):
    return [(i, (i + step) % n) for i in range(n)]


def island_parts(v):
    return [v] + [lax.ppermute(v, "x", ring(4, s)) for s in (1, 2, 3)]


def island_sum(v):
    a, b, c, d = island_parts(v)
    return (a + c) + (b + d)


def factor_into(gram, work):
    n = gram.shape[0]
    lane = lax.broadcasted_iota(jnp.int32, (n, 2 * n), 1)
    row_of = lax.broadcasted_iota(jnp.int32, (n, 2 * n), 0)
    work[:, :n] = gram
    work[:, n:] = jnp.where(lane[:, :n] == row_of[:, :n], 1.0, 0.0)
    below, across = row_of[:, :1], lane[:1]

    def pick(v, lanes, at):
        return jnp.sum(jnp.where(lanes == at, v, 0.0), axis=1, keepdims=True)

    def eliminate(step, carry):
        first = STEP * step
        state = work[...]
        rows = [work[pl.ds(first + i, 1), :] for i in range(STEP)]
        cols = [pick(state, lane, first + i) for i in range(STEP)]
        block = {
            (i, k): pick(rows[i], across, first + k) for i in range(STEP) for k in range(i, STEP)
        }
        for i in range(STEP):
            scale = 1.0 / block[i, i]
            for k in range(i + 1, STEP):
                ratio = block[i, k] * scale
                rows[k] = rows[k] - ratio * rows[i]
                cols[k] = cols[k] - ratio * cols[i]
                for m in range(k, STEP):
                    block[k, m] = block[k, m] - ratio * block[i, m]
            weight = jnp.where(below > first + i, cols[i] * scale, 0.0)
            state = state - weight * rows[i]
        work[...] = state
        return carry

    lax.fori_loop(0, n // STEP, eliminate, 0)
    state = work[...]
    pivots = jnp.sum(jnp.where(lane == row_of, state, 0.0), axis=1, keepdims=True)
    return state[:, n:] * lax.rsqrt(pivots)


def factor_kernel(gram_ref, out_ref, work):
    out_ref[...] = factor_into(gram_ref[...], work)


def inverse_factor(gram):
    n = gram.shape[0]
    return pl.pallas_call(
        factor_kernel,
        out_shape=jax.ShapeDtypeStruct((n, n), jnp.float32),
        scratch_shapes=[pltpu.VMEM((n, 2 * n), jnp.float32)],
        cost_estimate=pl.CostEstimate(
            flops=16 * 1024 * 1024, bytes_accessed=16 * 1024 * 1024, transcendentals=0
        ),
        name="factor",
    )(gram)


def tiles(v):
    r, w = v.shape
    return v.reshape(r // 8, 8, w // 128, 128).transpose(0, 2, 1, 3).reshape(-1, 8, 128)


def untile(v, r, w):
    return v.reshape(r // 8, w // 128, 8, 128).transpose(0, 2, 1, 3).reshape(r, w)


def swap(v):
    return lax.ppermute(v, "c", ring(2, 1))


def row_sum(near, far):
    near = near + swap(far)
    parts = tiles(near)
    own = jnp.sum(lax.all_to_all(parts, ROW, 0, 0), axis=0)
    full = lax.all_to_all(jnp.broadcast_to(own, parts.shape), ROW, 0, 0)
    return untile(full, *near.shape)


def combine_kernel(island_ref, core_ref, grad_ref, buffer_ref, top_ref, bottom_ref):
    both = grad_ref[...].astype(jnp.float32) + buffer_ref[...].astype(jnp.float32)
    combined = both.astype(jnp.bfloat16).astype(jnp.float32)
    split = top_ref.shape[0]
    top_ref[...] = combined[:split]
    bottom_ref[...] = combined[split:]


def combine_block(island, core, grad, buffer, width):
    rows = grad.shape[0]
    half = width // 2
    spec = pl.BlockSpec((rows, half), lambda h, i, c: (0, 2 * i[0] + lax.rem(c[0] + h, 2)))
    piece = pl.BlockSpec((rows // 2, half), lambda h, i, c: (0, h))
    shape = jax.ShapeDtypeStruct((rows // 2, width), jnp.float32)
    return pl.pallas_call(
        combine_kernel,
        out_shape=(shape, shape),
        grid_spec=pltpu.PrefetchScalarGridSpec(
            num_scalar_prefetch=2,
            grid=(2,),
            in_specs=[spec, spec],
            out_specs=(piece, piece),
        ),
        cost_estimate=pl.CostEstimate(
            flops=rows * width, bytes_accessed=rows * width * 8, transcendentals=0
        ),
        name="combine",
    )(island.reshape(1), core.reshape(1), grad, buffer)


def low_high(v):
    high = v.astype(jnp.bfloat16)
    return high, (v - high.astype(jnp.float32)).astype(jnp.bfloat16)


def finish_kernel(me_ref, core_ref, *refs):
    gram_refs, near_refs, refs = refs[:4], refs[4:8], refs[8:]
    far_ref, others_ref, inverse_ref, image_ref, combined_ref = refs[:5]
    far_refs = [far_ref] + [others_ref.at[i] for i in range(3)]
    rest = refs[5:]
    params_ref, momentum_ref, error_out, params_out, momentum_out = rest[:5]
    left4, mine4, right4, left, work = rest[5:]
    step = pl.program_id(0)
    width = right4.shape[1]
    half = width // 2
    quarter = params_ref.shape[0]
    islands = len(near_refs)

    @pl.when(step == 0)
    def _():
        a, b, c, d = [ref[...] for ref in gram_refs]
        last = factor_into((a + c) + (b + d), work)
        sketch = dot(inverse_ref[...], image_ref[...], 1, 0)
        left[...] = dot(dot(last, sketch, 1, 0), last, 0, 0) * (1.0 / islands)
        high, low = low_high(left[...])
        left4[...] = jnp.concatenate([high, high, low, low], axis=1)
        own = pl.ds(pl.multiple_of(me_ref[0] * quarter, 8), quarter)
        high, low = low_high(left[own, :])
        mine4[...] = jnp.concatenate([high, high, low, low], axis=1)

    near = pl.multiple_of(core_ref[0] * half, half)
    far = pl.multiple_of((1 - core_ref[0]) * half, half)
    for s in range(islands):

        @pl.when(step == s)
        def _(s=s):
            for ref, at in ((near_refs[s], near), (far_refs[s], far)):
                high, low = low_high(ref[...])
                right4[:, pl.ds(at, half)] = jnp.concatenate([high, low, high, low], axis=0)

    approx = jnp.dot(left4[...], right4[...], preferred_element_type=jnp.float32)
    island = lax.rem(me_ref[0] + islands - step, islands)
    columns = pl.ds(pl.multiple_of(island * width, width), width)
    combined = combined_ref[:, columns].astype(jnp.float32)
    error_out[...] = (combined - approx).astype(jnp.bfloat16)
    mine = jnp.dot(mine4[...], right4[...], preferred_element_type=jnp.float32)
    moved = momentum_coef * momentum_ref[...] + mine
    momentum_out[...] = moved
    params_out[...] = params_ref[...] - outer_rate * (mine + momentum_coef * moved)


def finish(me, core, grams, nears, far, others, inverse, image, combined, params, momentum):
    rows, cols = combined.shape
    quarter = params.shape[0]
    rank, half = nears[0].shape
    islands = len(nears)
    width = 2 * half

    def block(n):
        return pl.BlockSpec((n, width), lambda s, m, c: (0, lax.rem(m[0] + islands - s, islands)))

    whole = pl.BlockSpec(memory_space=pltpu.VMEM)
    state = jax.ShapeDtypeStruct(params.shape, jnp.float32)
    return pl.pallas_call(
        finish_kernel,
        out_shape=(jax.ShapeDtypeStruct((rows, cols), jnp.bfloat16), state, state),
        grid_spec=pltpu.PrefetchScalarGridSpec(
            num_scalar_prefetch=2,
            grid=(islands,),
            in_specs=[whole] * (5 + 2 * islands) + [block(quarter), block(quarter)],
            out_specs=(block(rows), block(quarter), block(quarter)),
            scratch_shapes=[
                pltpu.VMEM((rows, 4 * rank), jnp.bfloat16),
                pltpu.VMEM((quarter, 4 * rank), jnp.bfloat16),
                pltpu.VMEM((4 * rank, width), jnp.bfloat16),
                pltpu.VMEM((rows, rank), jnp.float32),
                pltpu.VMEM((rank, 2 * rank), jnp.float32),
            ],
        ),
        name="finish",
    )(
        me.reshape(1),
        core.reshape(1),
        *grams,
        *nears,
        far,
        others,
        inverse,
        image,
        combined,
        params,
        momentum,
    )


def start_sketch(basis, combined):
    rank = basis.shape[1]
    rest, pieces = basis, []
    for _ in range(3):
        piece = lax.reduce_precision(rest, exponent_bits=8, mantissa_bits=7)
        pieces.append(piece.astype(jnp.bfloat16))
        rest = rest - piece
    wide = lax.dot_general(
        jnp.concatenate(pieces, axis=1),
        combined,
        (((0,), (1,)), ((), ())),
        preferred_element_type=jnp.float32,
    )
    return wide[2 * rank :] + wide[rank : 2 * rank] + wide[:rank]


def hop(v, pairs):
    return lax.ppermute(v, "x", pairs)


def shards(pseudo_grad, error_buffer, basis_init, params, momentum):
    grad, buffer = pseudo_grad[0], error_buffer[0]
    rows, cols = grad.shape
    rank = basis_init.shape[1]
    islands = lax.axis_size("x")
    me = lax.axis_index("x")
    core = lax.axis_index("c")
    width = cols // islands
    half = width // 2

    blocks = {
        s: combine_block(lax.rem(me + s, islands), core, grad, buffer, width)
        for s in (2, 1, 3, 0)
    }
    up, down = ring(islands, 1), ring(islands, -1)
    relay_up = hop(blocks[2][0], up)
    relay_down = hop(blocks[2][1], down)
    from_below = hop(blocks[1][1], up)
    from_above = hop(blocks[3][0], down)
    top_below = hop(blocks[1][0] + relay_up, up)
    bottom_above = hop(blocks[3][1] + relay_down, down)
    both = grad.astype(jnp.float32) + buffer.astype(jnp.float32)
    combined = lax.reduce_precision(both, exponent_bits=8, mantissa_bits=7)
    combined = lax.optimization_barrier(combined.astype(jnp.bfloat16))
    part = start_sketch(basis_init, combined)
    image = island_sum(part)
    basis = lax.dynamic_slice_in_dim(basis_init, me * width, width, 0)
    basis = jnp.where(core == 0, basis, jnp.roll(basis, half, axis=0)).T
    side = rank // 2
    hold = lax.optimization_barrier

    top = hold(blocks[0][0] + from_above)
    bottom = hold(blocks[0][1] + from_below)
    split = top.shape[0]
    early = hold(dot(image[:, :split], top, 1, 0) + dot(image[:, split:], bottom, 1, 0))
    top_image, bottom_image = image[:, :split], image[:, split:]

    def late(columns):
        return (
            early[:, columns]
            + dot(top_image, top_below[:, columns], 1, 0)
            + dot(bottom_image, bottom_above[:, columns], 1, 0)
        )

    near_columns, far_columns = slice(0, half), slice(half, width)
    far_part = late(far_columns)
    near_part = hold(late(near_columns))
    near = row_sum(near_part, far_part)
    total_near, total_far = hold(
        tuple(
            jnp.concatenate(
                [top[:, c] + top_below[:, c], bottom[:, c] + bottom_above[:, c]], axis=0
            )
            for c in (near_columns, far_columns)
        )
    )

    def own_rows(basis):
        return lax.dynamic_slice_in_dim(basis, core * side, side, 0)

    def gram_whole(own):
        other = swap(own)
        first, second = jnp.where(core == 0, own, other), jnp.where(core == 0, other, own)
        return jnp.concatenate([first, second], axis=1)

    def raw_sum(image):
        far_part = dot(image, total_far, 1, 0)
        return row_sum(hold(dot(image, total_near, 1, 0)), far_part)

    def sweep(_, carry):
        near, basis_near, basis_far = carry[:3]
        far = swap(near)
        image = hold(dot(near, total_near, 1, 1))
        gram = hold(dot(near, own_rows(basis_near), 1, 1))
        image = image + dot(far, total_far, 1, 1)
        gram = gram + dot(far, own_rows(basis_far), 1, 1)
        summed = island_sum(jnp.concatenate([image, gram], axis=1))
        image = summed[:, :rows]
        raw = raw_sum(image)
        inverse = inverse_factor(gram_whole(summed[:, rows:]))
        basis_near = dot(inverse, near, 1, 0)
        basis_far = dot(inverse, far, 1, 0)
        near = dot(inverse, raw, 1, 0)
        return near, basis_near, basis_far, image, inverse

    square = jnp.zeros((rank, rank), jnp.float32)
    near, basis_near, basis_far, image, inverse = lax.fori_loop(
        1,
        ITERS,
        sweep,
        (near, basis[:, :half], basis[:, half:], jnp.zeros_like(image), square),
    )
    nears = island_parts(near)
    far = swap(near)
    gram = hold(dot(basis_near, near, 1, 1)) + dot(basis_far, far, 1, 1)
    grams = island_parts(gram)
    stacked = jnp.stack(nears[1:])
    others = swap(stacked)
    new_error, new_params, new_momentum = finish(
        me,
        core,
        grams,
        nears,
        far,
        others,
        inverse,
        image,
        combined,
        params,
        momentum,
    )
    return (new_error[None], new_params, new_momentum)


def solution(mesh):
    fine = Mesh(mesh.devices.reshape(4, 4, 8, 2), ("x", "y", "z", "c"))
    block = P("x", ROW + ("c",), None)
    state = P(ROW + ("c", "x"), None)
    return jax.shard_map(
        shards,
        mesh=fine,
        in_specs=(block, block, P(), state, state),
        out_specs=(block, state, state),
        check_vma=False,
    )
```
